32 devices in a mesh: row: 4 (over z), col: 8 (over y, x, core).
Axes of the slice: x: 2, y: 2, z: 4, core: 2. Of those that a mesh axis runs over, the one named last changes fastest.
Arguments:
- rhs: bfloat16 [4, 8, 128, 1024], P('row', 'col'), may hold values from -6 to 6
- operators: bfloat16 [4, 8, 3, 1024, 1024], P('row', 'col'), may hold values from -0.09375 to 0.09375
- positions: int32 [128], replicated, may hold values from 0 to 32767
- start_tick: int32 [128], replicated, may hold values from 0 to 7
Outputs:
- traces: bfloat16 [4, 8, 128, 1024], P('row', 'col')
The draws below stay inside these ranges and needn't reach their ends.
All inputs are finite; a program needn't handle non-finite values.
Results may differ from the reference program's by a relative error of at most 0.006.
Values may be sent and summed in bfloat16 or wider, within the bound.
No kernel may reach another device: no remote copies, remote signals or barrier semaphores. Data moves between devices by JAX's collectives and lax.ppermute only.
A program may use at most 64 MiB of HBM per device.

```python
import jax
import jax.numpy as jnp
from jax import lax

TRACE = 1024
BATCH = 128
TICKS = 8
TURN = 4
POINTS = 32768
N_ROW = 4
N_COL = 8


def set_ends(array, own_key, smallest, high):
    extent = array.shape
    place = [jax.random.randint(jax.random.fold_in(own_key, axis), (), 0, extent[axis]) for axis in range(len(extent))]
    array = array.at[tuple(place)].set(smallest)
    longest = extent.index(max(extent))
    place[longest] = (place[longest] + 1) % extent[longest]
    return array.at[tuple(place)].set(high)


def block_scale(own_key, extent, cuts, least, top_value):
    gain, own = 1.0, jax.random.fold_in(own_key, 6)
    for position, blocks in cuts:
        draws = jnp.exp(jax.random.uniform(jax.random.fold_in(own, position), (blocks,), jnp.float32, least / len(cuts), top_value / len(cuts)))
        gain = gain * jnp.repeat(draws, extent[position] // blocks).reshape([-1 if axis == position else 1 for axis in range(len(extent))])
    return gain


def bell_draw(own_key, shape, scale, most, split=(), kind=jnp.bfloat16):
    array = jax.random.normal(own_key, shape, jnp.float32) * scale
    if len(split) > 0:
        array = block_scale(own_key, shape, split, -0.22, 0.18) * array
    return jnp.clip(array, min=-most, max=most).astype(kind)


def setup_inputs(seed: int = 0) -> dict:
    key_list = jax.random.split(jax.random.key(seed), 5)
    rhs = bell_draw(key_list[0], (N_ROW, N_COL, BATCH, TRACE), 1.0, 6.0, ((0, 4), (1, 8)))
    operators = bell_draw(key_list[1], (N_ROW, N_COL, 3, TRACE, TRACE), (4 * TRACE) ** -0.5, 0.09375, ((0, 4), (1, 8)))
    positions = set_ends(jax.random.randint(key_list[2], (BATCH,), 0, POINTS), jax.random.fold_in(key_list[2], 1), 0, POINTS - 1).astype(jnp.int32)
    start_tick = set_ends(jax.random.randint(key_list[3], (BATCH,), 0, TICKS), jax.random.fold_in(key_list[3], 1), 0, TICKS - 1).astype(jnp.int32)
    return dict(rhs=rhs, operators=operators, positions=positions, start_tick=start_tick)


def move_rows(field, sign):
    blank = jnp.zeros_like(field[:1])
    if sign > 0:
        return jnp.concatenate([blank, field[:-1]], axis=0)
    return jnp.concatenate([field[1:], blank], axis=0)


def move_cols(field, sign):
    blank = jnp.zeros_like(field[:, :1])
    if sign > 0:
        return jnp.concatenate([blank, field[:, :-1]], axis=1)
    return jnp.concatenate([field[:, 1:], blank], axis=1)


def reference(rhs, operators, positions, start_tick):
    n_sub = N_ROW * N_COL
    flat_ops = operators.reshape(n_sub, 3, TRACE, TRACE)
    subdomain = lax.broadcasted_iota(jnp.int32, (n_sub, BATCH, TRACE), 0)
    unknown = lax.broadcasted_iota(jnp.int32, (n_sub, BATCH, TRACE), 2)
    target = (subdomain * TRACE + unknown) == positions.astype(jnp.int32)[None, :, None]
    source = rhs.reshape(n_sub, BATCH, TRACE).astype(jnp.float32) + 4.0 * target.astype(jnp.float32)
    traces = jnp.zeros((N_ROW, N_COL, BATCH, TRACE), jnp.bfloat16)

    def combine(pack):
        incoming, mats = pack
        summed = jnp.dot(incoming[0], mats[0], preferred_element_type=jnp.float32)
        summed = summed + jnp.dot(incoming[1], mats[1], preferred_element_type=jnp.float32)
        return summed + jnp.dot(incoming[2], mats[2], preferred_element_type=jnp.float32)

    for tick_index in range(TICKS):
        sign = 1 if tick_index < TURN else -1
        if tick_index == 0:
            summed = source
        else:
            from_row = move_rows(traces, sign)
            from_col = move_cols(traces, sign)
            diagonal_in = move_cols(from_row, sign)
            stacked = jnp.stack([from_row, from_col, diagonal_in], axis=2).reshape(n_sub, 3, BATCH, TRACE)
            summed = source + lax.map(combine, (stacked, flat_ops))
        running = (tick_index >= start_tick)[None, :, None]
        traces = jnp.where(running, summed, 0.0).astype(jnp.bfloat16).reshape(N_ROW, N_COL, BATCH, TRACE)
    return traces
```

```python
import jax
import jax.numpy as jnp
from jax import lax
from jax.sharding import PartitionSpec as P

TICKS = 8
AXES = ("row", "col")


def closed(route, rows, cols):
    every = [(r, c) for r in range(rows) for c in range(cols)]
    sources, targets = {a for a, _ in route}, {b for _, b in route}
    free = [p for p in every if p not in targets]
    for a in [p for p in every if p not in sources]:
        far = lambda b: (b == a, abs(b[0] - a[0]) + abs(b[1] // 2 - a[1] // 2), b[1] != a[1])
        b = min(free, key=far)
        free.remove(b)
        route = route + [(a, b)]
    return [(a[0] * cols + a[1], b[0] * cols + b[1]) for a, b in route if a != b]


def shift(block, dr, dc):
    rows, cols = lax.axis_size("row"), lax.axis_size("col")
    inside = lambda r, c: 0 <= r < rows and 0 <= c < cols
    every = [(r, c) for r in range(rows) for c in range(cols)]
    route = [((r, c), (r + dr, c + dc)) for r, c in every if inside(r + dr, c + dc)]
    return lax.ppermute(block, AXES, closed(route, rows, cols))


def body(rhs, operators, positions, start_tick):
    rows, cols = lax.axis_size("row"), lax.axis_size("col")
    batches, width = rhs.shape[2:]
    ops = operators[0, 0]
    i, j = lax.axis_index("row"), lax.axis_index("col")
    local_point = positions - (i * cols + j) * width
    column_ids = lax.broadcasted_iota(jnp.int32, (batches, width), 1)
    spike = (local_point[:, None] == column_ids).astype(jnp.float32)
    source = rhs[0, 0].astype(jnp.float32) + 4.0 * spike
    traces = jnp.where((0 >= start_tick)[:, None], source, 0.0).astype(jnp.bfloat16)
    turning = TICKS // 2
    for tick in range(1, TICKS):
        s = 1 if tick < turning else -1
        has_row = (i - s >= 0) & (i - s < rows)
        has_col = (j - s >= 0) & (j - s < cols)
        begun = start_tick < tick
        keep = lambda x, ok: jnp.where((begun & ok)[:, None], x, jnp.zeros_like(x))
        up = shift(traces, s, 0)
        left = shift(traces, 0, s)
        up, left = keep(up, has_row), keep(left, has_col)
        corner = keep(shift(up, 0, s), has_col)
        summed = source
        for mat, block in enumerate((up, left, corner)):
            summed = summed + jnp.dot(block, ops[mat], preferred_element_type=jnp.float32)
        running = (tick >= start_tick)[:, None]
        traces = jnp.where(running, summed, 0.0).astype(jnp.bfloat16)
    return traces[None, None]


def solution(mesh):
    placed = (P("row", "col", None, None), P("row", "col", None, None, None), P(), P())
    return jax.shard_map(
        body, mesh=mesh, in_specs=placed, out_specs=P("row", "col", None, None), check_vma=False
    )
```

```python
import functools

import jax
import jax.numpy as jnp
from jax import lax
from jax.experimental import pallas as pl
from jax.experimental.pallas import tpu as pltpu
from jax.sharding import PartitionSpec as P

TICKS = 8
AXES = ("row", "col")


def closed(route, rows, cols):
    every = [(r, c) for r in range(rows) for c in range(cols)]
    sources, targets = {a for a, _ in route}, {b for _, b in route}
    free = [p for p in every if p not in targets]
    for a in [p for p in every if p not in sources]:
        far = lambda b: (b == a, abs(b[0] - a[0]) + abs(b[1] // 2 - a[1] // 2), b[1] != a[1])
        b = min(free, key=far)
        free.remove(b)
        route = route + [(a, b)]
    return [(a[0] * cols + a[1], b[0] * cols + b[1]) for a, b in route if a != b]


def shift(block, dr, dc):
    rows, cols = lax.axis_size("row"), lax.axis_size("col")
    inside = lambda r, c: 0 <= r < rows and 0 <= c < cols
    every = [(r, c) for r in range(rows) for c in range(cols)]
    route = [((r, c), (r + dr, c + dc)) for r, c in every if inside(r + dr, c + dc)]
    return lax.ppermute(block, AXES, closed(route, rows, cols))


TILE = 16
SPARE = (1, 3)


def capacities(batches):
    part = lambda tick, spare: min(batches, -(-batches * tick // (TICKS * TILE)) * TILE + spare * TILE)
    levels = [tuple(part(tick, spare) for tick in range(1, TICKS)) for spare in SPARE]
    return levels + [(batches,) * (TICKS - 1)]


def resident(x):
    def kernel(x_ref, o_ref, sem):
        copy = pltpu.make_async_copy(x_ref, o_ref, sem)
        copy.start()
        copy.wait()

    return pl.pallas_call(
        kernel,
        out_shape=pltpu.VMEM(x.shape, x.dtype),
        in_specs=[pl.BlockSpec(memory_space=pl.ANY)],
        out_specs=pl.BlockSpec(memory_space=pltpu.VMEM),
        scratch_shapes=[pltpu.SemaphoreType.DMA],
        compiler_params=pltpu.CompilerParams(vmem_limit_bytes=1 << 20),
    )(x)


def exchange(block, s, form):
    up = shift(block, s, 0)
    if form == "G":
        corner = shift(block, s, s)
    left = shift(block, 0, s)
    if form == "D":
        corner = None
    return up, left, corner


def sweep(sizes):
    def run(traces, source, operators, start_tick, *seen):
        for tick in range(1, TICKS):
            s = 1 if tick < TICKS // 2 else -1
            has_row, has_col, has_both = seen[:3] if s > 0 else seen[3:]
            n = sizes[tick - 1]
            form = "G" if n <= 72 else "D"
            keep = lambda x, first: jnp.where((first[:n] < tick)[:, None], x, jnp.zeros_like(x))
            up, left, corner = exchange(traces[:n], s, form)
            if tick == 1:
                ops = resident(operators)
            up, left = keep(up, has_row), keep(left, has_col)
            if corner is None:
                corner = keep(shift(up, 0, s), has_col)
            else:
                corner = keep(corner, has_both)
            summed = source[:n]
            for mat, block in enumerate((up, left, corner)):
                summed = summed + jnp.dot(block, ops[mat], preferred_element_type=jnp.float32)
            if n < source.shape[0]:
                summed = jnp.concatenate([summed, source[n:]], axis=0)
            running = (tick >= start_tick)[:, None]
            traces = jnp.where(running, summed, 0.0).astype(jnp.bfloat16)
        return traces

    return run


def body(rhs, operators, positions, start_tick):
    rows, cols = lax.axis_size("row"), lax.axis_size("col")
    batches, width = rhs.shape[2:]
    i, j = lax.axis_index("row"), lax.axis_index("col")

    number = jnp.arange(batches, dtype=jnp.int32)
    key = start_tick * batches + number
    rank = jnp.sum((key[None, :] < key[:, None]).astype(jnp.int32), axis=1)
    chosen = rank[None, :] == number[:, None]
    place = chosen.astype(jnp.bfloat16)
    levels = capacities(batches)
    lost = [
        functools.reduce(jnp.logical_or, [(rank >= n) & (start_tick < tick) for tick, n in enumerate(sizes, 1)])
        for sizes in levels[:-1]
    ]
    level = jnp.max(sum(one.astype(jnp.int32) for one in lost))
    sort = lambda v: jnp.sum(jnp.where(chosen, v[None, :], 0), axis=1)
    start_tick, positions = sort(start_tick), sort(positions)

    local_point = positions - (i * cols + j) * width
    column_ids = lax.broadcasted_iota(jnp.int32, (batches, width), 1)
    spike = (local_point[:, None] == column_ids).astype(jnp.float32)
    source = jnp.dot(place, rhs[0, 0], preferred_element_type=jnp.float32) + 4.0 * spike
    traces = jnp.where((0 >= start_tick)[:, None], source, 0.0).astype(jnp.bfloat16)
    seen = {}
    for s in (1, -1):
        row_ok, col_ok = (i - s >= 0) & (i - s < rows), (j - s >= 0) & (j - s < cols)
        seen[s] = tuple(jnp.where(ok, start_tick, TICKS) for ok in (row_ok, col_ok, row_ok & col_ok))
    traces = lax.switch(
        level, [sweep(sizes) for sizes in levels], traces, source, operators[0, 0], start_tick, *seen[1], *seen[-1]
    )
    back = lax.dot_general(place, traces, (((0,), (0,)), ((), ())), preferred_element_type=jnp.float32)
    return back.astype(jnp.bfloat16)[None, None]


def solution(mesh):
    placed = (P("row", "col", None, None), P("row", "col", None, None, None), P(), P())
    return jax.shard_map(
        body, mesh=mesh, in_specs=placed, out_specs=P("row", "col", None, None), check_vma=False
    )
```
